32 devices in a mesh: dp: 4 (over z), gx: 4 (over x, core), gy: 2 (over y).
Axes of the slice: x: 2, y: 2, z: 4, core: 2. Of those that a mesh axis runs over, the one named last changes fastest.
Arguments:
- inputs: bfloat16 [4, 1024, 2048], P('dp', None, 'gx'), may hold values from -6 to 6
- lengths: int32 [4], P('dp'), may hold values from 256 to 1024, as said below
- grad_out: bfloat16 [4, 1024, 2048], P('dp', None, 'gx'), may hold values from -6 to 6
- gain_mix: float32 [2048], P('gx'), may hold values from 0.5 to 1.5
- input_weight: bfloat16 [2048, 2816], P('gx', 'gy'), may hold values from -0.125 to 0.125
- branch_weight: bfloat16 [2048, 2816], P('gx', 'gy'), may hold values from -0.125 to 0.125
- conv_w: float32 [4, 2816], P(None, 'gy'), may hold values from -3 to 3
- conv_b: float32 [2816], P('gy'), may hold values from -3 to 3
- gate_a: bfloat16 [16, 176, 176], P('gy'), may hold values from -0.4375 to 0.4375
- bias_a: float32 [2816], P('gy'), may hold values from -4 to 4
- gate_x: bfloat16 [16, 176, 176], P('gy'), may hold values from -0.4375 to 0.4375
- bias_x: float32 [2816], P('gy'), may hold values from -4 to 4
- lam: float32 [2816], P('gy'), may hold values from 2 to 7
- output_weight: bfloat16 [2816, 2048], P('gy', 'gx'), may hold values from -0.3125 to 0.3125
- gain_mlp: float32 [2048], P('gx'), may hold values from 0.5 to 1.5
- gate_weight: bfloat16 [2048, 6144], P('gx', 'gy'), may hold values from -0.125 to 0.125
- up_weight: bfloat16 [2048, 6144], P('gx', 'gy'), may hold values from -0.125 to 0.125
- down_weight: bfloat16 [6144, 2048], P('gy', 'gx'), may hold values from -0.125 to 0.125
Outputs:
- output: bfloat16 [4, 1024, 2048], P('dp', None, 'gx')
- grad_inputs: bfloat16 [4, 1024, 2048], P('dp', None, 'gx')
- grad_gain_mix: float32 [2048], P('gx')
- grad_w_in: float32 [2048, 2816], P('gx', 'gy')
- grad_w_branch: float32 [2048, 2816], P('gx', 'gy')
- grad_conv_w: float32 [4, 2816], P(None, 'gy')
- grad_conv_b: float32 [2816], P('gy')
- grad_gate_a: float32 [16, 176, 176], P('gy')
- grad_bias_a: float32 [2816], P('gy')
- grad_gate_x: float32 [16, 176, 176], P('gy')
- grad_bias_x: float32 [2816], P('gy')
- grad_lam: float32 [2816], P('gy')
- grad_w_out: float32 [2816, 2048], P('gy', 'gx')
- grad_gain_mlp: float32 [2048], P('gx')
- grad_w_g: float32 [2048, 6144], P('gx', 'gy')
- grad_w_u: float32 [2048, 6144], P('gx', 'gy')
- grad_w_d: float32 [6144, 2048], P('gy', 'gx')
- rms_out: float32 [], replicated
- rms_grad: float32 [], replicated
The draws below stay inside these ranges and needn't reach their ends.
Inputs may be any that keep to these rules, and one draw needn't show every extreme that they name: `lengths`: valid tokens of each sequence, a prefix of its 1024 slots; in every draw one sequence fills all 1024 slots and one has a quarter of them.
All inputs are finite; a program needn't handle non-finite values.
Results may differ from the reference program's by a relative error of at most 0.0095.
Values may be sent and summed in bfloat16 or wider, within the bound.
No kernel may reach another device: no remote copies, remote signals or barrier semaphores. Data moves between devices by JAX's collectives and lax.ppermute only.
A program may use at most 256 MiB of HBM per device.

```python
import jax
import jax.numpy as jnp
from jax import lax

D = 2048
R = 2816
NB = 16
BS = 176
CW = 4
F = 6144
LEN = 1024
SEQS = 4


def draw_lengths(key, part):
    drawn = jax.random.randint(key, (SEQS,), LEN // 4, LEN + 1, dtype=jnp.int32)
    drawn = drawn.at[0].set(LEN)
    return drawn.at[SEQS - 1].set(LEN // 4)


def block_levels(rng, shape, cuts, least, top_value):
    loudness, own = 1.0, jax.random.fold_in(rng, 6)
    for axis_at, parts in cuts:
        steps = jnp.exp(jax.random.uniform(jax.random.fold_in(own, axis_at), (parts,), jnp.float32, least / len(cuts), top_value / len(cuts)))
        loudness = loudness * jnp.repeat(steps, shape[axis_at] // parts).reshape([-1 if axis == axis_at else 1 for axis in range(len(shape))])
    return loudness


def scatter_about(key, dims, deviation, bound, split=(), kind=jnp.bfloat16):
    result = deviation * jax.random.normal(key, dims, jnp.float32)
    if split:
        result = result * block_levels(key, dims, split, -0.22, 0.18)
    return jnp.clip(result, -bound, bound).astype(kind)


def setup_inputs(seed: int = 0) -> dict:
    arg_keys = jax.random.split(jax.random.key(seed), 19)
    return {
        "inputs": scatter_about(arg_keys[0], (SEQS, LEN, D), 1.0, 6.0, ((0, 4), (2, 4))),
        "lengths": draw_lengths(jax.random.fold_in(arg_keys[18], 71), 0),
        "grad_out": scatter_about(arg_keys[2], (SEQS, LEN, D), 1.0, 6.0, ((0, 4), (2, 4))),
        "gain_mix": jnp.clip(1.0 + 0.1 * jax.random.normal(arg_keys[3], (D,), jnp.float32), 0.5, 1.5),
        "input_weight": scatter_about(arg_keys[4], (D, R), D ** -0.5, 0.125, ((0, 4), (1, 2))),
        "branch_weight": scatter_about(arg_keys[5], (D, R), D ** -0.5, 0.125, ((0, 4), (1, 2))),
        "conv_w": scatter_about(arg_keys[6], (CW, R), CW ** -0.5, 3.0, ((1, 2),), jnp.float32),
        "conv_b": scatter_about(arg_keys[7], (R,), 0.5, 3.0, ((0, 2),), jnp.float32),
        "gate_a": scatter_about(arg_keys[8], (NB, BS, BS), BS ** -0.5, 0.4375, ((0, 2),)),
        "bias_a": scatter_about(arg_keys[9], (R,), 1.0, 4.0, ((0, 2),), jnp.float32),
        "gate_x": scatter_about(arg_keys[10], (NB, BS, BS), BS ** -0.5, 0.4375, ((0, 2),)),
        "bias_x": scatter_about(arg_keys[11], (R,), 1.0, 4.0, ((0, 2),), jnp.float32),
        "lam": jnp.clip(2.0 + 5.0 * jax.random.uniform(arg_keys[12], (R,), jnp.float32) ** block_levels(arg_keys[12], (R,), ((0, 2),), -0.2, 0.2), 2.0, 7.0),
        "output_weight": scatter_about(arg_keys[13], (R, D), (R // 8) ** -0.5, 0.3125, ((0, 2), (1, 4))),
        "gain_mlp": jnp.clip(1.0 + 0.1 * jax.random.normal(arg_keys[14], (D,), jnp.float32), 0.5, 1.5),
        "gate_weight": scatter_about(arg_keys[15], (D, F), D ** -0.5, 0.125, ((0, 4), (1, 2))),
        "up_weight": scatter_about(arg_keys[16], (D, F), D ** -0.5, 0.125, ((0, 4), (1, 2))),
        "down_weight": scatter_about(arg_keys[17], (F, D), (F // 3) ** -0.5, 0.125, ((0, 2), (1, 4))),
    }


highest_precision = lax.Precision.HIGHEST
decay_power = 8.0
norm_eps = 1e-06

@jax.custom_vjp
def low(v):
    return lax.optimization_barrier(v.astype(jnp.bfloat16)).astype(jnp.float32)

@jax.custom_vjp
def low_back(v):
    return v

def low_keep(v):
    return (low(v), None)

def low_pass(kept, grad):
    return (grad,)

def back_keep(v):
    return (v, None)

def back_low(kept, grad):
    return (low(grad),)
low.defvjp(low_keep, low_pass)
low_back.defvjp(back_keep, back_low)

def smooth_gate(pre_act):
    return jax.nn.gelu(pre_act, approximate=True)

def linear_state(decay_rate, drive_term):

    def combine(earlier, later):
        return (earlier[0] * later[0], later[0] * earlier[1] + later[1])
    return lax.associative_scan(combine, (decay_rate, drive_term), axis=1)[1]

def rms_norm(values, gain_vec):
    scale_rows = lax.rsqrt(lax.optimization_barrier(jnp.mean(values * values, axis=-1, keepdims=True)) + norm_eps)
    return values * scale_rows * gain_vec

def forward(sequence, gain_mix, input_weight, branch_weight, conv_w, conv_b, gate_a, bias_a, gate_x, bias_x, lam, output_weight, gain_mlp, gate_weight, up_weight, down_weight):
    normalized_input = low(rms_norm(sequence, gain_mix))
    inner_projected = low_back(jnp.einsum('yen,nk->yek', normalized_input, input_weight, precision=highest_precision))
    gating_branch = low_back(jnp.einsum('yen,nk->yek', normalized_input, branch_weight, precision=highest_precision))
    padded = jnp.pad(inner_projected, ((0, 0), (CW - 1, 0), (0, 0)))
    conv_total = jnp.zeros_like(inner_projected) + conv_b
    for offset in range(CW):
        conv_total = conv_total + conv_w[offset] * padded[:, CW - 1 - offset:CW - 1 - offset + LEN]
    conv_low = low(conv_total)
    conv_blocks = conv_low.reshape(conv_low.shape[0], LEN, NB, BS)
    gate_pre = low_back(jnp.einsum('slnb,nbc->slnc', conv_blocks, gate_a, precision=highest_precision).reshape(conv_low.shape) + bias_a)
    input_pre = low_back(jnp.einsum('slnb,nbc->slnc', conv_blocks, gate_x, precision=highest_precision).reshape(conv_low.shape) + bias_x)
    log_decay = -decay_power * jax.nn.sigmoid(gate_pre) * jax.nn.softplus(-lam)
    decay_rate = jnp.exp(log_decay)
    drive_term = jnp.sqrt(-jnp.expm1(2.0 * log_decay)) * jax.nn.sigmoid(input_pre) * conv_low
    lru_state = linear_state(decay_rate, drive_term)
    mixer_result = low(smooth_gate(gating_branch) * lru_state)
    mixer_output = low_back(jnp.einsum('aqv,vc->aqc', mixer_result, output_weight, precision=highest_precision))
    middle_residual = sequence + mixer_output
    normalized_feedforward = low(rms_norm(middle_residual, gain_mlp))
    feedforward_gate = low_back(jnp.einsum('vyt,tr->vyr', normalized_feedforward, gate_weight, precision=highest_precision))
    feedforward_up = low_back(jnp.einsum('vyt,tr->vyr', normalized_feedforward, up_weight, precision=highest_precision))
    hidden_activation = low(smooth_gate(feedforward_gate) * feedforward_up)
    return middle_residual + low_back(jnp.einsum('qgr,ra->qga', hidden_activation, down_weight, precision=highest_precision))

def reference(inputs, lengths, grad_out, gain_mix, input_weight, branch_weight, conv_w, conv_b, gate_a, bias_a, gate_x, bias_x, lam, output_weight, gain_mlp, gate_weight, up_weight, down_weight):
    weights_f32 = tuple((weight.astype(jnp.float32) for weight in (gain_mix, input_weight, branch_weight, conv_w, conv_b, gate_a, bias_a, gate_x, bias_x, lam, output_weight, gain_mlp, gate_weight, up_weight, down_weight)))
    positions = jnp.arange(LEN, dtype=jnp.int32)

    def one_sequence(totals, seq_item):
        sequence, seq_length, cotangent = seq_item
        valid_rows = (positions < seq_length).astype(jnp.float32)[None, :, None]
        final, pullback = jax.vjp(forward, sequence.astype(jnp.float32)[None], *weights_f32)
        grad_list = pullback(cotangent.astype(jnp.float32)[None] * valid_rows)
        grad_seq = grad_list[0]
        square_sums = (jnp.sum(valid_rows * final * final), jnp.sum(valid_rows * grad_seq * grad_seq))
        totals = jax.tree.map(jnp.add, totals, (tuple(grad_list[1:]), square_sums))
        return (totals, (final[0].astype(jnp.bfloat16), grad_seq[0].astype(jnp.bfloat16)))
    start_totals = (tuple((jnp.zeros_like(weight) for weight in weights_f32)), (jnp.zeros((), jnp.float32), jnp.zeros((), jnp.float32)))
    totals, (outputs, grad_inputs) = lax.scan(one_sequence, start_totals, (inputs, lengths, grad_out))
    grad_list, square_sums = totals
    token_count = jnp.sum(lengths).astype(jnp.float32) * D
    rms_out = jnp.sqrt(square_sums[0] / token_count)
    rms_grad = jnp.sqrt(square_sums[1] / token_count)
    return (outputs, grad_inputs) + tuple(grad_list) + (rms_out, rms_grad)
```

```python
import jax
import jax.numpy as jnp
from jax import lax
from jax.experimental import pallas as pl
from jax.experimental.pallas import tpu as pltpu
from jax.sharding import PartitionSpec as P

bf16 = jnp.bfloat16
f32 = jnp.float32
SQRT_2_OVER_PI = 0.7978845608028654
CHUNKS = 8
STEP = 32


def expm1_neg(y):
    series = 1.0 + y * (1.0 / 9.0)
    for order in range(8, 1, -1):
        series = 1.0 + y * (1.0 / order) * series
    return jnp.where(y > -0.5, y * series, jnp.exp(y) - 1.0)


def gelu_parts(v):
    tanh_value = jnp.tanh(SQRT_2_OVER_PI * (v + 0.044715 * (v * v * v)))
    half = 0.5 * (1.0 + tanh_value)
    slope = half + 0.5 * v * (1.0 - tanh_value * tanh_value) * (
        SQRT_2_OVER_PI * (1.0 + 3.0 * 0.044715 * (v * v))
    )
    return v * half, slope


def gelu_value(v):
    return 0.5 * v * (1.0 + jnp.tanh(SQRT_2_OVER_PI * (v + 0.044715 * (v * v * v))))


LANES = 128


def slab_put(slabs, rows, values):
    width = values.shape[1]
    for j in range(slabs.shape[0]):
        size = min(LANES, width - j * LANES)
        slabs[j, rows, pl.ds(0, size)] = values[:, j * LANES : j * LANES + size]


def slab_get(slabs, rows, width):
    parts = []
    for j in range(slabs.shape[0]):
        parts.append(slabs[j, rows, pl.ds(0, min(LANES, width - j * LANES))])
    return jnp.concatenate(parts, axis=1)


def chunk_scan(order, rates, rate_shift, values, prefix, carries, width):
    slabs = range(values.shape[0])
    span = prefix.shape[1] // CHUNKS

    def advance(n, carry):
        hidden, product = carry
        s = n if order > 0 else span - 1 - n
        rows = pl.ds(s, CHUNKS, stride=span)
        rate_rows = pl.ds(s + rate_shift, CHUNKS, stride=span)
        next_hidden, next_product = [], []
        for j in slabs:
            rate = rates[j, rate_rows, :]
            next_hidden.append(rate * hidden[j] + values[j, rows, :])
            next_product.append(product[j] * rate)
            values[j, rows, :] = next_hidden[j]
            prefix[j, rows, :] = next_product[j]
        return tuple(next_hidden), tuple(next_product)

    zeros = tuple(jnp.zeros((CHUNKS, LANES), f32) for _ in slabs)
    ones = tuple(jnp.ones((CHUNKS, LANES), f32) for _ in slabs)
    hidden, product = lax.fori_loop(0, span, advance, (zeros, ones), unroll=8)
    for j in slabs:
        size = min(LANES, width - j * LANES)
        entering = jnp.zeros((1, LANES), f32)
        for c in range(CHUNKS) if order > 0 else range(CHUNKS - 1, -1, -1):
            carries[pl.ds(c, 1), pl.ds(j * LANES, size)] = entering[:, :size]
            entering = product[j][c : c + 1] * entering + hidden[j][c : c + 1]


def mixer_forward_kernel(
    joint_ref, tap_ref, conv_bias_ref, gate_a_ref, bias_a_ref, gate_x_ref, bias_x_ref, coef_ref,
    mixed_ref, conv_low_ref, sig_a_ref, sig_x_ref, decay_ref, root_ref, state_ref,
    inner_pad, rates, drive, prefix, carries,
):
    length, width = conv_low_ref.shape
    pitch = joint_ref.shape[1] // 2
    taps = tap_ref.shape[0]
    span = length // CHUNKS
    inner_pad[pl.ds(0, 8), :] = jnp.zeros((8, width), f32)
    inner_pad[pl.ds(8, length), :] = joint_ref[:, pl.ds(0, width)]

    def convolve(i, carry):
        start = pl.multiple_of(i * STEP, STEP)
        total = jnp.broadcast_to(conv_bias_ref[...], (STEP, width))
        window = inner_pad[pl.ds(start, STEP + 8), :]
        for k in range(taps):
            total = total + tap_ref[pl.ds(k, 1), :] * window[8 - k : 8 - k + STEP]
        conv_low_ref[pl.ds(start, STEP), :] = total.astype(bf16)
        return carry

    lax.fori_loop(0, length // STEP, convolve, 0)
    sig_a_ref[...] = jnp.dot(conv_low_ref[...], gate_a_ref[...], preferred_element_type=f32)
    sig_x_ref[...] = jnp.dot(conv_low_ref[...], gate_x_ref[...], preferred_element_type=f32)

    def gates(i, carry):
        rows = pl.ds(pl.multiple_of(i * STEP, STEP), STEP)
        sig_a = jax.nn.sigmoid(sig_a_ref[rows, :] + bias_a_ref[...])
        sig_x = jax.nn.sigmoid(sig_x_ref[rows, :] + bias_x_ref[...])
        log_decay = sig_a * coef_ref[...]
        root = jnp.sqrt(-expm1_neg(2.0 * log_decay))
        sig_a_ref[rows, :] = sig_a
        sig_x_ref[rows, :] = sig_x
        decay = jnp.exp(log_decay)
        decay_ref[rows, :] = decay
        slab_put(rates, rows, decay)
        root_ref[rows, :] = root
        slab_put(drive, rows, root * sig_x * conv_low_ref[rows, :].astype(f32))
        return carry

    lax.fori_loop(0, length // STEP, gates, 0)

    chunk_scan(1, rates, 0, drive, prefix, carries, width)

    def finish(i, carry):
        start = pl.multiple_of(i * STEP, STEP)
        rows = pl.ds(start, STEP)
        state = slab_get(drive, rows, width) + slab_get(prefix, rows, width) * carries[pl.ds(start // span, 1), :]
        state_ref[rows, :] = state
        mixed_ref[rows, :] = (gelu_value(joint_ref[rows, pl.ds(pitch, width)]) * state).astype(bf16)
        return carry

    lax.fori_loop(0, length // STEP, finish, 0)


def mixer_forward(joint, taps, conv_bias, gate_a, bias_a, gate_x, bias_x, coef):
    length, width = joint.shape[0], taps.shape[1]
    full = jax.ShapeDtypeStruct((length, width), f32)
    low = jax.ShapeDtypeStruct((length, width), bf16)
    slabs = pl.cdiv(width, LANES)
    return pl.pallas_call(
        mixer_forward_kernel,
        out_shape=(low, low, full, full, full, full, full),
        scratch_shapes=[
            pltpu.VMEM((length + 8, width), f32),
            pltpu.VMEM((slabs, length, LANES), f32),
            pltpu.VMEM((slabs, length, LANES), f32),
            pltpu.VMEM((slabs, length, LANES), f32),
            pltpu.VMEM((CHUNKS, width), f32),
        ],
        cost_estimate=pl.CostEstimate(
            flops=4 * length * width * width, bytes_accessed=32 * length * width, transcendentals=6 * length * width
        ),
        compiler_params=pltpu.CompilerParams(vmem_limit_bytes=48 * 1024 * 1024),
        name="mixer_forward",
    )(joint, taps, conv_bias, gate_a, bias_a, gate_x, bias_x, coef)


def mixer_backward_kernel(
    grad_mixed_ref, joint_ref, conv_low_ref, sig_a_ref, sig_x_ref, decay_ref, root_ref, state_ref,
    tap_ref, gate_a_ref, gate_x_ref, coef_ref, slope_ref,
    grad_joint_ref, gate_low_ref, input_low_ref, small_ref,
    inner_pad, state_pad, rates, gain, prefix, grad_conv, carries,
):
    length, width = conv_low_ref.shape
    pitch = joint_ref.shape[1] // 2
    taps = tap_ref.shape[0]
    span = length // CHUNKS
    steps = length // STEP
    zeros8 = jnp.zeros((8, width), f32)
    inner_pad[pl.ds(0, 8), :] = zeros8
    inner_pad[pl.ds(8, length), :] = joint_ref[:, pl.ds(0, width)]
    grad_joint_ref[...] = jnp.zeros(grad_joint_ref.shape, bf16)
    state_pad[pl.ds(0, 8), :] = zeros8
    slab_put(rates, pl.ds(length, 8), zeros8)
    grad_conv[pl.ds(length, 8), :] = zeros8

    def open_gate(i, carry):
        start = pl.multiple_of(i * STEP, STEP)
        rows = pl.ds(start, STEP)
        value, slope = gelu_parts(joint_ref[rows, pl.ds(pitch, width)])
        grad_mixed = grad_mixed_ref[rows, :]
        state = state_ref[rows, :]
        state_pad[pl.ds(start + 8, STEP), :] = state
        slab_put(rates, rows, decay_ref[rows, :])
        slab_put(gain, rows, grad_mixed * value)
        grad_joint_ref[rows, pl.ds(pitch, width)] = (grad_mixed * state * slope).astype(bf16)
        return carry

    lax.fori_loop(0, steps, open_gate, 0)

    chunk_scan(-1, rates, 1, gain, prefix, carries, width)

    def fold(values):
        return jnp.sum(values.reshape(STEP // 8, 8, width), axis=0)

    def gates(i, sums):
        start = pl.multiple_of(i * STEP, STEP)
        rows = pl.ds(start, STEP)
        q = slab_get(gain, rows, width) + slab_get(prefix, rows, width) * carries[pl.ds(start // span, 1), :]
        sig_a = sig_a_ref[rows, :]
        sig_x = sig_x_ref[rows, :]
        decay = decay_ref[rows, :]
        root = root_ref[rows, :]
        conv = conv_low_ref[rows, :].astype(f32)
        earlier = state_pad[pl.ds(start, STEP + 8), :][7 : 7 + STEP]
        g = q * (earlier * decay - sig_x * conv * (decay * decay) / root)
        rate = q * root
        gate_low = (g * coef_ref[...] * (sig_a * (1.0 - sig_a))).astype(bf16)
        input_low = (rate * conv * (sig_x * (1.0 - sig_x))).astype(bf16)
        gate_low_ref[rows, :] = gate_low
        input_low_ref[rows, :] = input_low
        grad_conv[rows, :] = rate * sig_x
        sum_a, sum_x, sum_lam = sums
        return (
            sum_a + fold(gate_low.astype(f32)),
            sum_x + fold(input_low.astype(f32)),
            sum_lam + fold(sig_a * g),
        )

    sum_a, sum_x, sum_lam = lax.fori_loop(0, steps, gates, (zeros8, zeros8, zeros8))
    contract = (((1,), (1,)), ((), ()))
    grad_conv[pl.ds(0, length), :] += lax.dot_general(
        gate_low_ref[...], gate_a_ref[...], contract, preferred_element_type=f32
    )
    grad_conv[pl.ds(0, length), :] += lax.dot_general(
        input_low_ref[...], gate_x_ref[...], contract, preferred_element_type=f32
    )

    def convolve(i, sums):
        start = pl.multiple_of(i * STEP, STEP)
        ahead = grad_conv[pl.ds(start, STEP + 8), :]
        behind = inner_pad[pl.ds(start, STEP + 8), :]
        here = ahead[:STEP]
        total = jnp.zeros((STEP, width), f32)
        out = []
        for k in range(taps):
            total = total + tap_ref[pl.ds(k, 1), :] * ahead[k : k + STEP]
            out.append(sums[k] + fold(here * behind[8 - k : 8 - k + STEP]))
        out.append(sums[taps] + fold(here))
        grad_joint_ref[pl.ds(start, STEP), pl.ds(0, width)] = total.astype(bf16)
        return tuple(out)

    sums = lax.fori_loop(0, steps, convolve, (zeros8,) * (taps + 1))
    for k in range(taps + 1):
        small_ref[pl.ds(k, 1), :] = jnp.sum(sums[k], axis=0, keepdims=True)
    small_ref[pl.ds(taps + 1, 1), :] = jnp.sum(sum_a, axis=0, keepdims=True)
    small_ref[pl.ds(taps + 2, 1), :] = jnp.sum(sum_x, axis=0, keepdims=True)
    small_ref[pl.ds(taps + 3, 1), :] = jnp.sum(sum_lam, axis=0, keepdims=True) * slope_ref[...]


def mixer_backward(
    grad_mixed, joint, conv_low, sig_a, sig_x, decay, root, state, taps, gate_a, gate_x, coef, slope
):
    length, width = conv_low.shape
    low = jax.ShapeDtypeStruct((length, width), bf16)
    slabs = pl.cdiv(width, LANES)
    return pl.pallas_call(
        mixer_backward_kernel,
        out_shape=(jax.ShapeDtypeStruct(joint.shape, bf16), low, low, jax.ShapeDtypeStruct((taps.shape[0] + 4, width), f32)),
        scratch_shapes=[pltpu.VMEM((length + 8, width), f32)] * 2
        + [pltpu.VMEM((slabs, length + 8, LANES), f32)]
        + [pltpu.VMEM((slabs, length, LANES), f32)] * 2
        + [pltpu.VMEM((length + 8, width), f32), pltpu.VMEM((CHUNKS, width), f32)],
        cost_estimate=pl.CostEstimate(
            flops=4 * length * width * width, bytes_accessed=40 * length * width, transcendentals=2 * length * width
        ),
        compiler_params=pltpu.CompilerParams(vmem_limit_bytes=56 * 1024 * 1024),
        name="mixer_backward",
    )(grad_mixed, joint, conv_low, sig_a, sig_x, decay, root, state, taps, gate_a, gate_x, coef, slope)


norm_eps = 1e-06
decay_power = 8.0


def exchange(value, flip, across=False):
    wide, high = lax.axis_size("gx"), lax.axis_size("gy")
    if not across:
        return lax.ppermute(value, "gx", [(i, i ^ flip) for i in range(wide)])
    if flip == 0:
        return lax.ppermute(value, "gy", [(j, j ^ 1) for j in range(high)])
    return lax.ppermute(
        value,
        ("gx", "gy"),
        [(i * high + j, (i ^ flip) * high + (j ^ 1)) for i in range(wide) for j in range(high)],
    )


def line_gather(value, place, buffer):
    count = lax.axis_size("dp")
    here = lax.axis_index("dp")
    rightward, leftward = [value], [value]
    for _ in range(count - 1):
        rightward.append(lax.ppermute(rightward[-1], "dp", [(i, i + 1) for i in range(count - 1)]))
        leftward.append(lax.ppermute(leftward[-1], "dp", [(i + 1, i) for i in range(count - 1)]))
    buffer = place(buffer, value, here)
    for s in range(1, count):
        arrived = jnp.where(here >= s, rightward[s], leftward[count - s])
        buffer = place(buffer, arrived, jnp.where(here >= s, here - s, here - s + count))
    return buffer


def line_sum(value):
    count = lax.axis_size("dp")
    here = lax.axis_index("dp")
    kind = value.dtype
    if count == 1:
        return value
    half = count // 2
    for s in range(half - 1):
        arrived = lax.ppermute(value, "dp", [(s, s + 1), (count - 1 - s, count - 2 - s)])
        value = (value.astype(f32) + arrived.astype(f32)).astype(kind)
    arrived = lax.ppermute(value, "dp", [(half - 1, half), (half, half - 1)])
    value = (value.astype(f32) + arrived.astype(f32)).astype(kind)
    for s in range(half - 1):
        arrived = lax.ppermute(value, "dp", [(half - 1 - s, half - 2 - s), (half + s, half + s + 1)])
        takes = jnp.logical_or(here == half - 2 - s, here == half + s + 1)
        value = jnp.where(takes, arrived, value)
    return value


def in_order(pieces):
    place = lax.axis_index("gx")
    count = len(pieces)
    bit = 1
    while bit < count:
        swapped = jnp.bitwise_and(place, bit) != 0
        pieces = [jnp.where(swapped, pieces[r ^ bit], pieces[r]) for r in range(count)]
        bit *= 2
    return pieces


def halves(mine, other):
    side = lax.axis_index("gy")
    return jnp.where(
        side == 0, jnp.concatenate([mine, other], axis=0), jnp.concatenate([other, mine], axis=0)
    )


def my_half(values, other=False):
    rows = values.shape[0] // lax.axis_size("gy")
    side = lax.axis_index("gy")
    return lax.dynamic_slice_in_dim(values, ((1 - side) if other else side) * rows, rows, 0)


def plane_scatter(pieces):
    low = [p.astype(bf16) for p in pieces]
    kept = pieces[0] + exchange(low[1], 1).astype(f32)
    passed = (pieces[2] + exchange(low[3], 1).astype(f32)).astype(bf16)
    side = exchange(my_half(kept, other=True).astype(bf16), 0, across=True)
    along = exchange(my_half(passed), 2)
    corner = exchange(my_half(passed, other=True), 2, across=True)
    return (my_half(kept) + side.astype(f32)) + (along.astype(f32) + corner.astype(f32))


def plane_gather(block):
    along, side, corner = exchange(block, 2), exchange(block, 0, across=True), exchange(block, 2, across=True)
    mate, mate_along = exchange(block, 1), exchange(along, 1)
    mate_side, mate_corner = exchange(side, 1), exchange(corner, 1)
    return jnp.concatenate(
        [halves(block, side), halves(mate, mate_side), halves(along, corner), halves(mate_along, mate_corner)],
        axis=1,
    )


def row_total(values):
    return ((values + exchange(values, 1)) + exchange(values, 2)) + exchange(values, 3)


def dot(left, right, left_dim=1, right_dim=0):
    return lax.dot_general(
        left, right, (((left_dim,), (right_dim,)), ((), ())), preferred_element_type=f32
    )


def spread_weight(cut, buffer, put, parts):
    place = lax.axis_index("gx")
    member = lax.axis_index("dp")
    rows = parts // lax.axis_size("dp")
    far = [
        exchange(cut(jnp.bitwise_xor(place, r), member * rows, rows), r) for r in (2, 3)
    ]
    buffer = put(buffer, cut(place, 0, parts), 0, 0)
    buffer = put(buffer, exchange(cut(jnp.bitwise_xor(place, 1), 0, parts), 1), 1, 0)

    def put_both(held, value, index):
        held = put(held, value[0], 2, index * rows)
        return put(held, value[1], 3, index * rows)

    return line_gather(jnp.stack(far), put_both, buffer)


def send_home(pieces):
    pieces = [p.astype(bf16) for p in pieces]
    arrived = [pieces[0]] + [exchange(pieces[r], r) for r in range(1, len(pieces))]
    return in_order([line_sum(p).astype(f32) for p in arrived])


def place_part(part_value, full_shape, offset, axis_dim):
    return lax.dynamic_update_slice_in_dim(jnp.zeros(full_shape, f32), part_value, offset, axis_dim)


def body(
    inputs,
    lengths,
    grad_out,
    gain_mix,
    input_weight,
    branch_weight,
    conv_w,
    conv_b,
    gate_a,
    bias_a,
    gate_x,
    bias_x,
    lam,
    output_weight,
    gain_mlp,
    gate_weight,
    up_weight,
    down_weight,
):
    groups = lax.axis_size("gx")
    column = lax.axis_index("gx")
    length, wide = inputs.shape[1], inputs.shape[2]
    model = wide * groups
    mix_part = input_weight.shape[1] // groups
    feed_part = gate_weight.shape[1] // groups
    block_part = gate_a.shape[0] // groups
    block_size = gate_a.shape[1]
    pitch = pl.cdiv(mix_part, LANES) * LANES
    channel_start = column * mix_part
    block_start = column * block_part
    cols = [slice(r * wide, (r + 1) * wide) for r in range(groups)]

    own = inputs[0]
    far = exchange(own, 2)
    raw = jnp.concatenate([own, exchange(own, 1), far, exchange(far, 1)], axis=1)

    def cut_columns(weight, size):
        return lambda g, start, rows: lax.dynamic_slice(weight, (start, g * size), (rows, size))

    def cut_rows(weight, size):
        return lambda g, start, rows: lax.dynamic_slice(weight, (g * size + start, 0), (rows, weight.shape[1]))

    def put_rows(lane):
        return lambda held, value, r, row: lax.dynamic_update_slice(held, value, (r * wide + row, lane))

    def put_columns(held, value, r, row):
        return lax.dynamic_update_slice(held, value, (row, r * wide))

    joint_weight = jnp.zeros((model, 2 * pitch), bf16)
    joint_weight = spread_weight(cut_columns(input_weight, mix_part), joint_weight, put_rows(0), wide)
    joint_weight = spread_weight(cut_columns(branch_weight, mix_part), joint_weight, put_rows(pitch), wide)
    out_weight = spread_weight(
        cut_rows(output_weight, mix_part), jnp.zeros((mix_part, model), bf16), put_columns, mix_part
    )
    feed_weight = jnp.zeros((model, 2 * feed_part), bf16)
    feed_weight = spread_weight(cut_columns(gate_weight, feed_part), feed_weight, put_rows(0), wide)
    feed_weight = spread_weight(cut_columns(up_weight, feed_part), feed_weight, put_rows(feed_part), wide)
    last_weight = spread_weight(
        cut_rows(down_weight, feed_part), jnp.zeros((feed_part, model), bf16), put_columns, feed_part
    )
    gains = jnp.stack([gain_mix, gain_mlp])
    gains = jnp.concatenate([gains] + [exchange(gains, r) for r in range(1, groups)], axis=1)

    valid_rows = (lax.broadcasted_iota(jnp.int32, (length, 1), 0) < lengths[0]).astype(f32)
    cotangent = grad_out[0]
    far = exchange(cotangent, 2)
    cotangent_full = jnp.concatenate([cotangent, exchange(cotangent, 1), far, exchange(far, 1)], axis=1)
    grad_low = (cotangent_full.astype(f32) * valid_rows).astype(bf16)

    def normalize(values, gain_vec):
        values = values.astype(f32)
        scale_rows = lax.rsqrt(jnp.sum(values * values, axis=1, keepdims=True) / model + norm_eps)
        return (values * scale_rows * gain_vec).astype(bf16), scale_rows

    normed_mix, scale_mix = normalize(raw, gains[0])
    joint = dot(normed_mix, joint_weight)

    def channels(values):
        return lax.dynamic_slice_in_dim(values, channel_start, mix_part, values.ndim - 1)

    def diagonal(blocks):
        blocks = lax.dynamic_slice_in_dim(blocks, block_start, block_part, 0)
        dense = jnp.zeros((mix_part, mix_part), bf16)
        for n in range(block_part):
            dense = lax.dynamic_update_slice(dense, blocks[n], (n * block_size, n * block_size))
        return dense

    taps = channels(conv_w)
    lam_part = channels(lam)[None]
    gate_a_part, gate_x_part = diagonal(gate_a), diagonal(gate_x)
    coef = -decay_power * jax.nn.softplus(-lam_part)
    slope = decay_power * jax.nn.sigmoid(-lam_part)
    mixed, conv_low, sig_a, sig_x, decay, root, state = mixer_forward(
        joint,
        taps,
        channels(conv_b)[None],
        gate_a_part,
        channels(bias_a)[None],
        gate_x_part,
        channels(bias_x)[None],
        coef,
    )
    middle = my_half(own).astype(f32) + plane_scatter([dot(mixed, out_weight[:, c]) for c in cols])

    middle_full = plane_gather(middle.astype(bf16))
    normed_mlp, scale_mlp_full = normalize(middle_full, gains[1])
    feed = dot(normed_mlp, feed_weight)
    gate_value, up_value = feed[:, :feed_part], feed[:, feed_part:]
    grad_hidden = dot(grad_low, last_weight, 1, 1)
    gate_act, gate_slope = gelu_parts(gate_value)
    hidden = (gate_act * up_value).astype(bf16)
    grad_feed = jnp.concatenate(
        [(grad_hidden * up_value * gate_slope).astype(bf16), (grad_hidden * gate_act).astype(bf16)], axis=1
    )
    grad_down = send_home([dot(hidden, grad_low[:, c], 0, 0) for c in cols])
    grad_gate = send_home([dot(normed_mlp[:, c], grad_feed[:, :feed_part], 0, 0) for c in cols])
    grad_up = send_home([dot(normed_mlp[:, c], grad_feed[:, feed_part:], 0, 0) for c in cols])
    grad_normed_mlp = plane_scatter([dot(grad_feed, feed_weight[c], 1, 1) for c in cols])

    unit_mlp = middle * my_half(scale_mlp_full)
    grad_top = my_half(cotangent).astype(f32) * my_half(valid_rows)
    scaled = grad_normed_mlp * gain_mlp
    project = row_total(jnp.sum(scaled * unit_mlp, axis=1)) / model
    grad_middle = grad_top + my_half(scale_mlp_full) * (scaled - unit_mlp * project[:, None])
    gain_mlp_part = jnp.sum(grad_normed_mlp * unit_mlp, axis=0)

    grad_mid_full = plane_gather(grad_middle.astype(bf16))
    grad_mixed = dot(grad_mid_full, out_weight, 1, 1)
    grad_output = send_home([dot(mixed, grad_mid_full[:, c], 0, 0) for c in cols])
    grad_joint, gate_low, input_low, small = mixer_backward(
        grad_mixed, joint, conv_low, sig_a, sig_x, decay, root, state, taps, gate_a_part, gate_x_part, coef, slope
    )
    grad_normed_mix = plane_scatter([dot(grad_joint, joint_weight[c], 1, 1) for c in cols])
    grad_joint_weight = send_home([dot(normed_mix[:, c], grad_joint, 0, 0) for c in cols])

    residual = my_half(own).astype(f32)
    scale_half = my_half(scale_mix)
    unit_mix = residual * scale_half
    scaled = grad_normed_mix * gain_mix
    project = row_total(jnp.sum(scaled * unit_mix, axis=1)) / model
    grad_x = grad_middle + scale_half * (scaled - unit_mix * project[:, None])
    gain_mix_part = jnp.sum(grad_normed_mix * unit_mix, axis=0)

    final = middle + plane_scatter([dot(hidden, last_weight[:, c]) for c in cols])
    output = final.astype(bf16)
    output = halves(output, exchange(output, 0, across=True))[None]
    grad_inputs = grad_x.astype(bf16)
    grad_inputs = halves(grad_inputs, exchange(grad_inputs, 0, across=True))[None]

    gate_blocks = []
    for low in (gate_low, input_low):
        dense = dot(conv_low, low, 0, 0)
        for n in range(block_part):
            span = slice(n * block_size, (n + 1) * block_size)
            gate_blocks.append(dense[span, span])
    gate_blocks = line_sum(jnp.stack(gate_blocks).astype(bf16))
    gate_blocks = in_order([gate_blocks] + [exchange(gate_blocks, r) for r in range(1, groups)])
    gate_blocks = jnp.stack(gate_blocks).astype(f32).reshape(groups, 2, block_part, block_size, block_size)
    grad_gate_a = gate_blocks[:, 0].reshape(gate_a.shape)
    grad_gate_x = gate_blocks[:, 1].reshape(gate_x.shape)
    half_valid = my_half(valid_rows)
    first = jnp.logical_and(column == 0, lax.axis_index("gy") == 0)
    stat_sums = jnp.stack(
        [
            jnp.sum(half_valid * final * final),
            jnp.sum(half_valid * grad_x * grad_x),
            jnp.where(first, jnp.sum(lengths).astype(f32), 0.0),
        ]
    )
    small = lax.psum(place_part(small, (small.shape[0], conv_w.shape[1]), channel_start, 1), ("dp", "gx"))
    grad_gains = lax.psum(jnp.stack([gain_mix_part, gain_mlp_part]), ("dp", "gy"))
    totals = lax.psum(stat_sums, ("dp", "gx", "gy"))
    token_count = totals[2] * model
    taps_count = conv_w.shape[0]

    def joint_columns(start):
        return jnp.concatenate([p[:, start : start + mix_part] for p in grad_joint_weight], axis=1)

    return (
        output,
        grad_inputs,
        grad_gains[0],
        joint_columns(0),
        joint_columns(pitch),
        small[:taps_count],
        small[taps_count],
        grad_gate_a,
        small[taps_count + 1],
        grad_gate_x,
        small[taps_count + 2],
        small[taps_count + 3],
        jnp.concatenate(grad_output, axis=0),
        grad_gains[1],
        jnp.concatenate(grad_gate, axis=1),
        jnp.concatenate(grad_up, axis=1),
        jnp.concatenate(grad_down, axis=0),
        jnp.sqrt(totals[0] / token_count),
        jnp.sqrt(totals[1] / token_count),
    )


def solution(mesh):
    placed = (
        P("dp", None, "gx"),
        P("dp"),
        P("dp", None, "gx"),
        P("gx"),
        P("gx", "gy"),
        P("gx", "gy"),
        P(None, "gy"),
        P("gy"),
        P("gy", None, None),
        P("gy"),
        P("gy", None, None),
        P("gy"),
        P("gy"),
        P("gy", "gx"),
        P("gx"),
        P("gx", "gy"),
        P("gx", "gy"),
        P("gy", "gx"),
    )
    return jax.shard_map(
        body,
        mesh=mesh,
        in_specs=placed,
        out_specs=(
            P("dp", None, "gx"),
            P("dp", None, "gx"),
            P("gx"),
            P("gx", "gy"),
            P("gx", "gy"),
            P(None, "gy"),
            P("gy"),
            P("gy", None, None),
            P("gy"),
            P("gy", None, None),
            P("gy"),
            P("gy"),
            P("gy", "gx"),
            P("gx"),
            P("gx", "gy"),
            P("gx", "gy"),
            P("gy", "gx"),
            P(),
            P(),
        ),
        check_vma=False,
    )
```

```python
import jax
import jax.numpy as jnp
from jax import lax
from jax.experimental import pallas as pl
from jax.experimental.pallas import tpu as pltpu
from jax.sharding import PartitionSpec as P

bf16 = jnp.bfloat16
f32 = jnp.float32
SQRT_2_OVER_PI = 0.7978845608028654
CHUNKS = 8
STEP = 32


def expm1_neg(y):
    series = 1.0 + y * (1.0 / 9.0)
    for order in range(8, 1, -1):
        series = 1.0 + y * (1.0 / order) * series
    return jnp.where(y > -0.5, y * series, jnp.exp(y) - 1.0)


def gelu_parts(v):
    tanh_value = jnp.tanh(SQRT_2_OVER_PI * (v + 0.044715 * (v * v * v)))
    half = 0.5 * (1.0 + tanh_value)
    slope = half + 0.5 * v * (1.0 - tanh_value * tanh_value) * (
        SQRT_2_OVER_PI * (1.0 + 3.0 * 0.044715 * (v * v))
    )
    return v * half, slope


def gelu_value(v):
    return 0.5 * v * (1.0 + jnp.tanh(SQRT_2_OVER_PI * (v + 0.044715 * (v * v * v))))


LANES = 128


def slab_put(slabs, rows, values):
    width = values.shape[1]
    for j in range(slabs.shape[0]):
        size = min(LANES, width - j * LANES)
        slabs[j, rows, pl.ds(0, size)] = values[:, j * LANES : j * LANES + size]


def slab_get(slabs, rows, width):
    parts = []
    for j in range(slabs.shape[0]):
        parts.append(slabs[j, rows, pl.ds(0, min(LANES, width - j * LANES))])
    return jnp.concatenate(parts, axis=1)


def chunk_scan(order, rates, rate_shift, values, prefix, carries, width):
    slabs = range(values.shape[0])
    span = prefix.shape[1] // CHUNKS

    def advance(n, carry):
        hidden, product = carry
        s = n if order > 0 else span - 1 - n
        rows = pl.ds(s, CHUNKS, stride=span)
        rate_rows = pl.ds(s + rate_shift, CHUNKS, stride=span)
        next_hidden, next_product = [], []
        for j in slabs:
            rate = rates[j, rate_rows, :]
            next_hidden.append(rate * hidden[j] + values[j, rows, :])
            next_product.append(product[j] * rate)
            values[j, rows, :] = next_hidden[j]
            prefix[j, rows, :] = next_product[j]
        return tuple(next_hidden), tuple(next_product)

    zeros = tuple(jnp.zeros((CHUNKS, LANES), f32) for _ in slabs)
    ones = tuple(jnp.ones((CHUNKS, LANES), f32) for _ in slabs)
    hidden, product = lax.fori_loop(0, span, advance, (zeros, ones), unroll=8)
    for j in slabs:
        size = min(LANES, width - j * LANES)
        entering = jnp.zeros((1, LANES), f32)
        for c in range(CHUNKS) if order > 0 else range(CHUNKS - 1, -1, -1):
            carries[pl.ds(c, 1), pl.ds(j * LANES, size)] = entering[:, :size]
            entering = product[j][c : c + 1] * entering + hidden[j][c : c + 1]


def mixer_forward_kernel(
    joint_ref, tap_ref, conv_bias_ref, gate_a_ref, bias_a_ref, gate_x_ref, bias_x_ref, coef_ref,
    mixed_ref, conv_low_ref, sig_a_ref, sig_x_ref, decay_ref, root_ref, state_ref,
    inner_pad, rates, drive, prefix, carries,
):
    length, width = conv_low_ref.shape
    pitch = joint_ref.shape[1] // 2
    taps = tap_ref.shape[0]
    span = length // CHUNKS
    inner_pad[pl.ds(0, 8), :] = jnp.zeros((8, width), f32)
    inner_pad[pl.ds(8, length), :] = joint_ref[:, pl.ds(0, width)]

    def convolve(i, carry):
        start = pl.multiple_of(i * STEP, STEP)
        total = jnp.broadcast_to(conv_bias_ref[...], (STEP, width))
        window = inner_pad[pl.ds(start, STEP + 8), :]
        for k in range(taps):
            total = total + tap_ref[pl.ds(k, 1), :] * window[8 - k : 8 - k + STEP]
        conv_low_ref[pl.ds(start, STEP), :] = total.astype(bf16)
        return carry

    lax.fori_loop(0, length // STEP, convolve, 0)
    sig_a_ref[...] = jnp.dot(conv_low_ref[...], gate_a_ref[...], preferred_element_type=f32)
    sig_x_ref[...] = jnp.dot(conv_low_ref[...], gate_x_ref[...], preferred_element_type=f32)

    def gates(i, carry):
        rows = pl.ds(pl.multiple_of(i * STEP, STEP), STEP)
        sig_a = jax.nn.sigmoid(sig_a_ref[rows, :] + bias_a_ref[...])
        sig_x = jax.nn.sigmoid(sig_x_ref[rows, :] + bias_x_ref[...])
        log_decay = sig_a * coef_ref[...]
        root = jnp.sqrt(-expm1_neg(2.0 * log_decay))
        sig_a_ref[rows, :] = sig_a
        sig_x_ref[rows, :] = sig_x
        decay = jnp.exp(log_decay)
        decay_ref[rows, :] = decay
        slab_put(rates, rows, decay)
        root_ref[rows, :] = root
        slab_put(drive, rows, root * sig_x * conv_low_ref[rows, :].astype(f32))
        return carry

    lax.fori_loop(0, length // STEP, gates, 0)

    chunk_scan(1, rates, 0, drive, prefix, carries, width)

    def finish(i, carry):
        start = pl.multiple_of(i * STEP, STEP)
        rows = pl.ds(start, STEP)
        state = slab_get(drive, rows, width) + slab_get(prefix, rows, width) * carries[pl.ds(start // span, 1), :]
        state_ref[rows, :] = state
        mixed_ref[rows, :] = (gelu_value(joint_ref[rows, pl.ds(pitch, width)]) * state).astype(bf16)
        return carry

    lax.fori_loop(0, length // STEP, finish, 0)


def mixer_forward(joint, taps, conv_bias, gate_a, bias_a, gate_x, bias_x, coef):
    length, width = joint.shape[0], taps.shape[1]
    full = jax.ShapeDtypeStruct((length, width), f32)
    low = jax.ShapeDtypeStruct((length, width), bf16)
    slabs = pl.cdiv(width, LANES)
    return pl.pallas_call(
        mixer_forward_kernel,
        out_shape=(low, low, full, full, full, full, full),
        scratch_shapes=[
            pltpu.VMEM((length + 8, width), f32),
            pltpu.VMEM((slabs, length, LANES), f32),
            pltpu.VMEM((slabs, length, LANES), f32),
            pltpu.VMEM((slabs, length, LANES), f32),
            pltpu.VMEM((CHUNKS, width), f32),
        ],
        cost_estimate=pl.CostEstimate(
            flops=4 * length * width * width, bytes_accessed=32 * length * width, transcendentals=6 * length * width
        ),
        compiler_params=pltpu.CompilerParams(vmem_limit_bytes=48 * 1024 * 1024),
        name="mixer_forward",
    )(joint, taps, conv_bias, gate_a, bias_a, gate_x, bias_x, coef)


def mixer_backward_kernel(
    grad_mixed_ref, joint_ref, conv_low_ref, sig_a_ref, sig_x_ref, decay_ref, root_ref, state_ref,
    tap_ref, gate_a_ref, gate_x_ref, coef_ref, slope_ref,
    grad_joint_ref, gate_low_ref, input_low_ref, small_ref,
    inner_pad, state_pad, rates, gain, prefix, grad_conv, carries,
):
    length, width = conv_low_ref.shape
    pitch = joint_ref.shape[1] // 2
    taps = tap_ref.shape[0]
    span = length // CHUNKS
    steps = length // STEP
    zeros8 = jnp.zeros((8, width), f32)
    inner_pad[pl.ds(0, 8), :] = zeros8
    inner_pad[pl.ds(8, length), :] = joint_ref[:, pl.ds(0, width)]
    grad_joint_ref[...] = jnp.zeros(grad_joint_ref.shape, bf16)
    state_pad[pl.ds(0, 8), :] = zeros8
    slab_put(rates, pl.ds(length, 8), zeros8)
    grad_conv[pl.ds(length, 8), :] = zeros8

    def open_gate(i, carry):
        start = pl.multiple_of(i * STEP, STEP)
        rows = pl.ds(start, STEP)
        value, slope = gelu_parts(joint_ref[rows, pl.ds(pitch, width)])
        grad_mixed = grad_mixed_ref[rows, :]
        state = state_ref[rows, :]
        state_pad[pl.ds(start + 8, STEP), :] = state
        slab_put(rates, rows, decay_ref[rows, :])
        slab_put(gain, rows, grad_mixed * value)
        grad_joint_ref[rows, pl.ds(pitch, width)] = (grad_mixed * state * slope).astype(bf16)
        return carry

    lax.fori_loop(0, steps, open_gate, 0)

    chunk_scan(-1, rates, 1, gain, prefix, carries, width)

    def fold(values):
        return jnp.sum(values.reshape(STEP // 8, 8, width), axis=0)

    def gates(i, sums):
        start = pl.multiple_of(i * STEP, STEP)
        rows = pl.ds(start, STEP)
        q = slab_get(gain, rows, width) + slab_get(prefix, rows, width) * carries[pl.ds(start // span, 1), :]
        sig_a = sig_a_ref[rows, :]
        sig_x = sig_x_ref[rows, :]
        decay = decay_ref[rows, :]
        root = root_ref[rows, :]
        conv = conv_low_ref[rows, :].astype(f32)
        earlier = state_pad[pl.ds(start, STEP + 8), :][7 : 7 + STEP]
        g = q * (earlier * decay - sig_x * conv * (decay * decay) / root)
        rate = q * root
        gate_low = (g * coef_ref[...] * (sig_a * (1.0 - sig_a))).astype(bf16)
        input_low = (rate * conv * (sig_x * (1.0 - sig_x))).astype(bf16)
        gate_low_ref[rows, :] = gate_low
        input_low_ref[rows, :] = input_low
        grad_conv[rows, :] = rate * sig_x
        sum_a, sum_x, sum_lam = sums
        return (
            sum_a + fold(gate_low.astype(f32)),
            sum_x + fold(input_low.astype(f32)),
            sum_lam + fold(sig_a * g),
        )

    sum_a, sum_x, sum_lam = lax.fori_loop(0, steps, gates, (zeros8, zeros8, zeros8))
    contract = (((1,), (1,)), ((), ()))
    grad_conv[pl.ds(0, length), :] += lax.dot_general(
        gate_low_ref[...], gate_a_ref[...], contract, preferred_element_type=f32
    )
    grad_conv[pl.ds(0, length), :] += lax.dot_general(
        input_low_ref[...], gate_x_ref[...], contract, preferred_element_type=f32
    )

    def convolve(i, sums):
        start = pl.multiple_of(i * STEP, STEP)
        ahead = grad_conv[pl.ds(start, STEP + 8), :]
        behind = inner_pad[pl.ds(start, STEP + 8), :]
        here = ahead[:STEP]
        total = jnp.zeros((STEP, width), f32)
        out = []
        for k in range(taps):
            total = total + tap_ref[pl.ds(k, 1), :] * ahead[k : k + STEP]
            out.append(sums[k] + fold(here * behind[8 - k : 8 - k + STEP]))
        out.append(sums[taps] + fold(here))
        grad_joint_ref[pl.ds(start, STEP), pl.ds(0, width)] = total.astype(bf16)
        return tuple(out)

    sums = lax.fori_loop(0, steps, convolve, (zeros8,) * (taps + 1))
    for k in range(taps + 1):
        small_ref[pl.ds(k, 1), :] = jnp.sum(sums[k], axis=0, keepdims=True)
    small_ref[pl.ds(taps + 1, 1), :] = jnp.sum(sum_a, axis=0, keepdims=True)
    small_ref[pl.ds(taps + 2, 1), :] = jnp.sum(sum_x, axis=0, keepdims=True)
    small_ref[pl.ds(taps + 3, 1), :] = jnp.sum(sum_lam, axis=0, keepdims=True) * slope_ref[...]


def mixer_backward(
    grad_mixed, joint, conv_low, sig_a, sig_x, decay, root, state, taps, gate_a, gate_x, coef, slope
):
    length, width = conv_low.shape
    low = jax.ShapeDtypeStruct((length, width), bf16)
    slabs = pl.cdiv(width, LANES)
    return pl.pallas_call(
        mixer_backward_kernel,
        out_shape=(jax.ShapeDtypeStruct(joint.shape, bf16), low, low, jax.ShapeDtypeStruct((taps.shape[0] + 4, width), f32)),
        scratch_shapes=[pltpu.VMEM((length + 8, width), f32)] * 2
        + [pltpu.VMEM((slabs, length + 8, LANES), f32)]
        + [pltpu.VMEM((slabs, length, LANES), f32)] * 2
        + [pltpu.VMEM((length + 8, width), f32), pltpu.VMEM((CHUNKS, width), f32)],
        cost_estimate=pl.CostEstimate(
            flops=4 * length * width * width, bytes_accessed=40 * length * width, transcendentals=2 * length * width
        ),
        compiler_params=pltpu.CompilerParams(vmem_limit_bytes=56 * 1024 * 1024),
        name="mixer_backward",
    )(grad_mixed, joint, conv_low, sig_a, sig_x, decay, root, state, taps, gate_a, gate_x, coef, slope)


norm_eps = 1e-06
decay_power = 8.0


def exchange(value, flip, across=False):
    wide, high = lax.axis_size("gx"), lax.axis_size("gy")
    if not across:
        return lax.ppermute(value, "gx", [(i, i ^ flip) for i in range(wide)])
    if flip == 0:
        return lax.ppermute(value, "gy", [(j, j ^ 1) for j in range(high)])
    return lax.ppermute(
        value,
        ("gx", "gy"),
        [(i * high + j, (i ^ flip) * high + (j ^ 1)) for i in range(wide) for j in range(high)],
    )


def after(value, *earlier):
    return lax.optimization_barrier((value,) + earlier)[0] if earlier else value


def line_sum(value):
    count = lax.axis_size("dp")
    here = lax.axis_index("dp")
    kind = value.dtype
    if count == 1:
        return value, value
    half = count // 2
    first = None
    for s in range(half - 1):
        arrived = lax.ppermute(value, "dp", [(s, s + 1), (count - 1 - s, count - 2 - s)])
        first = arrived if first is None else first
        value = (value.astype(f32) + arrived.astype(f32)).astype(kind)
    arrived = lax.ppermute(value, "dp", [(half - 1, half), (half, half - 1)])
    first = arrived if first is None else first
    value = (value.astype(f32) + arrived.astype(f32)).astype(kind)
    for s in range(half - 1):
        arrived = lax.ppermute(value, "dp", [(half - 1 - s, half - 2 - s), (half + s, half + s + 1)])
        takes = jnp.logical_or(here == half - 2 - s, here == half + s + 1)
        value = jnp.where(takes, arrived, value)
    return value, first


def joined(mine, other, mine_first, axis=0):
    return jnp.where(
        mine_first, jnp.concatenate([mine, other], axis=axis), jnp.concatenate([other, mine], axis=axis)
    )


def halves(mine, other):
    return joined(mine, other, lax.axis_index("gy") == 0)


def my_half(values, other=False):
    rows = values.shape[0] // lax.axis_size("gy")
    side = lax.axis_index("gy")
    return lax.dynamic_slice_in_dim(values, ((1 - side) if other else side) * rows, rows, 0)


def widen(own):
    near = exchange(my_half(own), 2)
    even = jnp.concatenate([own, halves(near, exchange(near, 0, across=True))], axis=1)
    return even, exchange(even, 1)


def plane_scatter(even, odd):
    wide = even.shape[1] // 2
    total = even + exchange(odd.astype(bf16), 1).astype(f32)
    kept, passed = total[:, :wide], total[:, wide:].astype(bf16)
    along = exchange(my_half(passed), 2)
    side = exchange(my_half(kept, other=True).astype(bf16), 0, across=True)
    corner = exchange(my_half(passed, other=True), 2, across=True)
    return (my_half(kept) + side.astype(f32)) + (along.astype(f32) + corner.astype(f32))


def plane_gather(block):
    along, side, corner = exchange(block, 2), exchange(block, 0, across=True), exchange(block, 2, across=True)
    even = halves(jnp.concatenate([block, along], axis=1), jnp.concatenate([side, corner], axis=1))
    return jnp.concatenate([even, exchange(even, 1)], axis=1), along


def row_total(values):
    values = values + exchange(values, 1)
    return values + exchange(values, 2)


def dot(left, right, left_dim=1, right_dim=0):
    return lax.dot_general(
        left, right, (((left_dim,), (right_dim,)), ((), ())), preferred_element_type=f32
    )


def from_neighbour(own, far):
    if lax.axis_size("dp") % 2:
        return exchange(far, 2), None
    near = exchange(far, 2)
    member = lax.axis_index("dp")
    pairs = [(i, i ^ 1) for i in range(lax.axis_size("dp"))]
    return near, lambda value: joined(value, lax.ppermute(value, "dp", pairs), member % 2 == 0)


def chip_cut(weight, axis, neighbour):
    size = 2 * (weight.shape[axis] // lax.axis_size("gx"))
    place = lax.axis_index("gx") // 2
    return lax.dynamic_slice_in_dim(weight, ((1 - place) if neighbour else place) * size, size, axis)


def dp_half(values):
    if lax.axis_size("dp") % 2:
        return values
    rows = values.shape[0] // 2
    return lax.dynamic_slice_in_dim(values, (lax.axis_index("dp") % 2) * rows, rows, 0)


def core_cut(values, axis, mate):
    size = values.shape[axis] // 2
    core = lax.axis_index("gx") % 2
    return lax.dynamic_slice_in_dim(values, ((1 - core) if mate else core) * size, size, axis)


def in_order(own, mate, near, near_mate, axis):
    place = lax.axis_index("gx")
    core_first, chip_first = place % 2 == 0, place // 2 == 0
    return joined(joined(own, mate, core_first, axis), joined(near, near_mate, core_first, axis), chip_first, axis)


def body(
    inputs,
    lengths,
    grad_out,
    gain_mix,
    input_weight,
    branch_weight,
    conv_w,
    conv_b,
    gate_a,
    bias_a,
    gate_x,
    bias_x,
    lam,
    output_weight,
    gain_mlp,
    gate_weight,
    up_weight,
    down_weight,
):
    groups = lax.axis_size("gx")
    column = lax.axis_index("gx")
    length, wide = inputs.shape[1], inputs.shape[2]
    model = wide * groups
    half = model // 2
    mix_part = input_weight.shape[1] // groups
    feed_part = gate_weight.shape[1] // groups
    block_part = gate_a.shape[0] // groups
    block_size = gate_a.shape[1]
    pitch = pl.cdiv(mix_part, LANES) * LANES
    channel_start = column * mix_part
    block_start = column * block_part
    own = inputs[0]

    def far_columns(weights):
        return jnp.concatenate([dp_half(chip_cut(w, 1, True)) for w in weights], axis=1)

    joint_far, joint_fill = from_neighbour(None, far_columns([input_weight, branch_weight]))
    raw_even, raw_odd = widen(own)
    out_far, out_fill = from_neighbour(None, dp_half(chip_cut(output_weight, 0, True)))
    feed_far, feed_fill = from_neighbour(None, far_columns([gate_weight, up_weight]))
    last_far, last_fill = from_neighbour(None, dp_half(chip_cut(down_weight, 0, True)))
    gains = jnp.stack([gain_mix, gain_mlp])
    gains = jnp.concatenate([gains, exchange(gains, 2)], axis=1)
    gains = jnp.concatenate([gains, exchange(gains, 1)], axis=1)

    def fill(far, filler):
        return filler(far) if filler is not None else far

    def column_weight(weights, far, filler, pitch):
        far = fill(far, filler)
        near = jnp.concatenate([chip_cut(w, 1, False) for w in weights], axis=1)
        both = jnp.concatenate([near, far], axis=0)
        size = both.shape[1] // len(weights)

        def cut(mate):
            parts = [core_cut(both[:, n * size : (n + 1) * size], 1, mate) for n in range(len(weights))]
            parts = [jnp.pad(p, ((0, 0), (0, pitch - p.shape[1]))) for p in parts]
            return jnp.concatenate(parts, axis=1)

        return jnp.concatenate([cut(False), exchange(cut(True), 1)], axis=0)

    def row_weight(weight, far, filler):
        both = jnp.concatenate([chip_cut(weight, 0, False), fill(far, filler)], axis=1)
        return jnp.concatenate([core_cut(both, 0, False), exchange(core_cut(both, 0, True), 1)], axis=1)

    joint_weight = column_weight([input_weight, branch_weight], joint_far, joint_fill, pitch)
    out_weight = row_weight(output_weight, out_far, out_fill)

    def normalize(values, gain_vec):
        values = values.astype(f32)
        scale_rows = lax.rsqrt(jnp.sum(values * values, axis=1, keepdims=True) / model + norm_eps)
        return (values * scale_rows * gain_vec).astype(bf16), scale_rows

    normed_mix, scale_mix = normalize(jnp.concatenate([raw_even, raw_odd], axis=1), gains[0])
    joint = dot(normed_mix, joint_weight)

    def channels(values):
        return lax.dynamic_slice_in_dim(values, channel_start, mix_part, values.ndim - 1)

    def diagonal(blocks):
        blocks = lax.dynamic_slice_in_dim(blocks, block_start, block_part, 0)
        dense = jnp.zeros((mix_part, mix_part), bf16)
        for n in range(block_part):
            dense = lax.dynamic_update_slice(dense, blocks[n], (n * block_size, n * block_size))
        return dense

    taps = channels(conv_w)
    lam_part = channels(lam)[None]
    gate_a_part, gate_x_part = diagonal(gate_a), diagonal(gate_x)
    coef = -decay_power * jax.nn.softplus(-lam_part)
    slope = decay_power * jax.nn.sigmoid(-lam_part)
    mixed, conv_low, sig_a, sig_x, decay, root, state = mixer_forward(
        joint,
        taps,
        channels(conv_b)[None],
        gate_a_part,
        channels(bias_a)[None],
        gate_x_part,
        channels(bias_x)[None],
        coef,
    )
    middle = my_half(own).astype(f32) + plane_scatter(
        dot(mixed, out_weight[:, :half]), dot(mixed, out_weight[:, half:])
    )

    feed_weight = column_weight([gate_weight, up_weight], after(feed_far, mixed), feed_fill, feed_part)
    last_weight = row_weight(down_weight, after(last_far, mixed), last_fill)
    valid_rows = (lax.broadcasted_iota(jnp.int32, (length, 1), 0) < lengths[0]).astype(f32)
    cotangent = grad_out[0]
    wide_cotangent = jnp.concatenate(widen(after(cotangent, mixed)), axis=1)
    grad_low = (wide_cotangent.astype(f32) * valid_rows).astype(bf16)

    middle_full, _ = plane_gather(middle.astype(bf16))
    normed_mlp, scale_mlp_full = normalize(middle_full, gains[1])
    feed = dot(normed_mlp, feed_weight)
    gate_value, up_value = feed[:, :feed_part], feed[:, feed_part:]
    grad_hidden = dot(grad_low, last_weight, 1, 1)
    gate_act, gate_slope = gelu_parts(gate_value)
    hidden = (gate_act * up_value).astype(bf16)
    grad_gate = (grad_hidden * up_value * gate_slope).astype(bf16)
    grad_up = (grad_hidden * gate_act).astype(bf16)
    grad_feed = jnp.concatenate([grad_gate, grad_up], axis=1)
    grad_normed_mlp = plane_scatter(
        dot(grad_feed, feed_weight[:half], 1, 1), dot(grad_feed, feed_weight[half:], 1, 1)
    )

    unit_mlp = middle * my_half(scale_mlp_full)
    grad_top = my_half(cotangent).astype(f32) * my_half(valid_rows)
    scaled = grad_normed_mlp * gain_mlp
    project = row_total(jnp.sum(scaled * unit_mlp, axis=1)) / model
    grad_middle = grad_top + my_half(scale_mlp_full) * (scaled - unit_mlp * project[:, None])
    gain_mlp_part = jnp.sum(grad_normed_mlp * unit_mlp, axis=0)

    grad_mid_full, gathered = plane_gather(grad_middle.astype(bf16))
    grad_mixed = dot(grad_mid_full, out_weight, 1, 1)
    grad_joint, gate_low, input_low, small = mixer_backward(
        grad_mixed, joint, conv_low, sig_a, sig_x, decay, root, state, taps, gate_a_part, gate_x_part, coef, slope
    )
    grad_normed_mix = plane_scatter(
        dot(grad_joint, joint_weight[:half], 1, 1), dot(grad_joint, joint_weight[half:], 1, 1)
    )
    residual = my_half(own).astype(f32)
    scale_half = my_half(scale_mix)
    unit_mix = residual * scale_half
    scaled = grad_normed_mix * gain_mix
    project = row_total(jnp.sum(scaled * unit_mix, axis=1)) / model
    grad_x = grad_middle + scale_half * (scaled - unit_mix * project[:, None])
    gain_mix_part = jnp.sum(grad_normed_mix * unit_mix, axis=0)

    def pieces(left, right, axis):
        both = []
        for side in range(2):
            part = []
            for n in range(2):
                cols = slice((2 * side + n) * wide, (2 * side + n + 1) * wide)
                part.append(
                    dot(left[:, cols], right, 0, 0) if axis == 0 else dot(left, right[:, cols], 0, 0)
                )
            both.append(jnp.stack(part).astype(bf16))
        return both

    def home(left, right, axis, *earlier):
        even, odd = pieces(left, right, axis)
        mate = exchange(odd, 1)
        near = jnp.stack([even[0], mate[0]])
        far = exchange(after(jnp.stack([even[1], mate[1]]), *earlier), 2)
        return near, far

    down_near, down_far = home(hidden, grad_low, 1, gathered)
    gate_near, gate_far = home(normed_mlp, grad_gate, 0, gathered, down_far)
    up_near, up_far = home(normed_mlp, grad_up, 0, gathered, gate_far)
    out_near, out_far = home(mixed, grad_mid_full, 1)
    joint_near, joint_far = home(normed_mix, grad_joint, 0)
    chunks = [
        down_near, gate_near, up_near, down_far, gate_far, up_far, out_near, out_far, joint_near, joint_far,
    ]
    sums, starts = [], []
    for n, chunk in enumerate(chunks):
        total, first = line_sum(after(chunk, starts[n - 2]) if n >= 2 else chunk)
        sums.append(total)
        starts.append(first)

    def owned(near, far, axis):
        near, far = near.astype(f32), far.astype(f32)
        return in_order(near[0], near[1], far[0], far[1], axis)

    grad_w_d = owned(sums[0], sums[3], 0)
    grad_w_g = owned(sums[1], sums[4], 1)
    grad_w_u = owned(sums[2], sums[5], 1)
    grad_w_out = owned(sums[6], sums[7], 0)

    def joint_columns(start):
        cols = slice(start, start + mix_part)
        return owned(sums[8][:, :, cols], sums[9][:, :, cols], 1)

    late_hidden = after(hidden, gathered)
    final = middle + plane_scatter(
        dot(late_hidden, last_weight[:, :half]), dot(late_hidden, last_weight[:, half:])
    )
    output = final.astype(bf16)
    output = halves(output, exchange(output, 0, across=True))[None]
    grad_inputs = grad_x.astype(bf16)
    grad_inputs = halves(grad_inputs, exchange(grad_inputs, 0, across=True))[None]

    gate_blocks = []
    for low in (gate_low, input_low):
        dense = dot(conv_low, low, 0, 0)
        for n in range(block_part):
            span = slice(n * block_size, (n + 1) * block_size)
            gate_blocks.append(dense[span, span])
    gate_blocks, _ = line_sum(jnp.stack(gate_blocks).astype(bf16))
    gate_pair = jnp.stack([gate_blocks, exchange(gate_blocks, 1)])
    gate_far = exchange(gate_pair, 2)
    gate_all = in_order(gate_pair[:1], gate_pair[1:], gate_far[:1], gate_far[1:], 0).astype(f32)
    gate_all = gate_all.reshape(groups, 2, block_part, block_size, block_size)
    grad_gate_a = gate_all[:, 0].reshape(gate_a.shape)
    grad_gate_x = gate_all[:, 1].reshape(gate_x.shape)

    half_valid = my_half(valid_rows)
    tokens = jnp.where(lax.axis_index("gy") == 0, lengths[0].astype(f32), 0.0)
    stats = [jnp.sum(half_valid * final * final), jnp.sum(half_valid * grad_x * grad_x), tokens]
    shared = jnp.stack([gain_mix_part, gain_mlp_part] + [jnp.full((wide,), v, f32) for v in stats])
    shared = shared + exchange(shared, 0, across=True)
    small_rows = small.shape[0]
    packed = jnp.concatenate([jnp.pad(small, ((0, 0), (0, wide - mix_part))), shared], axis=0)
    packed, _ = line_sum(packed)
    packed_pair = jnp.stack([packed, exchange(packed, 1)])
    packed_far = exchange(packed_pair, 2)
    totals = (packed_pair[0, :, 0] + packed_pair[1, :, 0]) + (packed_far[0, :, 0] + packed_far[1, :, 0])
    small_pair, small_far = packed_pair[:, :small_rows, :mix_part], packed_far[:, :small_rows, :mix_part]
    small = in_order(small_pair[0], small_pair[1], small_far[0], small_far[1], 1)
    token_count = (totals[small_rows + 4] / groups) * model
    taps_count = conv_w.shape[0]

    return (
        output,
        grad_inputs,
        packed[small_rows],
        joint_columns(0),
        joint_columns(pitch),
        small[:taps_count],
        small[taps_count],
        grad_gate_a,
        small[taps_count + 1],
        grad_gate_x,
        small[taps_count + 2],
        small[taps_count + 3],
        grad_w_out,
        packed[small_rows + 1],
        grad_w_g,
        grad_w_u,
        grad_w_d,
        jnp.sqrt(totals[small_rows + 2] / token_count),
        jnp.sqrt(totals[small_rows + 3] / token_count),
    )


def solution(mesh):
    placed = (
        P("dp", None, "gx"),
        P("dp"),
        P("dp", None, "gx"),
        P("gx"),
        P("gx", "gy"),
        P("gx", "gy"),
        P(None, "gy"),
        P("gy"),
        P("gy", None, None),
        P("gy"),
        P("gy", None, None),
        P("gy"),
        P("gy"),
        P("gy", "gx"),
        P("gx"),
        P("gx", "gy"),
        P("gx", "gy"),
        P("gy", "gx"),
    )
    return jax.shard_map(
        body,
        mesh=mesh,
        in_specs=placed,
        out_specs=(
            P("dp", None, "gx"),
            P("dp", None, "gx"),
            P("gx"),
            P("gx", "gy"),
            P("gx", "gy"),
            P(None, "gy"),
            P("gy"),
            P("gy", None, None),
            P("gy"),
            P("gy", None, None),
            P("gy"),
            P("gy"),
            P("gy", "gx"),
            P("gx"),
            P("gx", "gy"),
            P("gx", "gy"),
            P("gy", "gx"),
            P(),
            P(),
        ),
        check_vma=False,
    )
```
